32 devices in a mesh: grp: 4 (over z), col: 8 (over y, x, core).
Axes of the slice: x: 2, y: 2, z: 4, core: 2. Of those that a mesh axis runs over, the one named last changes fastest.
Arguments:
- inverse: bfloat16 [4, 8192, 8192], P('grp', None, 'col'), as said below
- right_side: float32 [4, 8192, 256], P('grp', 'col'), may hold values from -6 to 6
- penalty: float32 [256], replicated, may hold values from 0.2 to 6
Outputs:
- consensus: float32 [8192, 256], P('col')
- duals: float32 [4, 8192, 256], P('grp', 'col')
The draws below stay inside these ranges and needn't reach their ends.
Inputs may be any that keep to these rules, and one draw needn't show every extreme that they name: Each inverse[g] is symmetric.
All inputs are finite; a program needn't handle non-finite values.
Results may differ from the reference program's by a relative error of at most 0.0042.
Values may be sent and summed in bfloat16 or wider, within the bound.
A program may use at most 64 MiB of HBM per device.

```python
import math
import jax
import jax.numpy as jnp
from jax import lax

K = 8192
PATHS = 256
ITERS = 3
GROUPS = 4


def draw_inverse(key, part):

    def draw_group(member):
        member_key = jax.random.fold_in(key, member)
        noise_key, diagonal_key = jax.random.split(member_key, 2)
        noise = jax.random.normal(noise_key, (K, K), jnp.float32)
        symmetric = (noise + noise.T) * (0.35 / math.sqrt(2.0 * K))
        diagonal = jax.random.uniform(diagonal_key, (K,), jnp.float32, 0.9, 1.6)
        position = lax.iota(jnp.int32, K)
        matrix = jnp.where(position[:, None] == position[None, :], diagonal[None, :], symmetric)
        return matrix.astype(jnp.bfloat16)
    return lax.map(draw_group, jnp.arange(GROUPS, dtype=jnp.int32))


def block_levels(rng, shape, pieces, smallest, high):
    def one(dim, shards_of):
        heights = jax.random.uniform(jax.random.fold_in(jax.random.fold_in(rng, 6), dim), (shards_of,), jnp.float32, smallest / len(pieces), high / len(pieces))
        return jnp.repeat(jnp.exp(heights), shape[dim] // shards_of).reshape((-1,) + (1,) * (len(shape) - dim - 1))

    gain = one(*pieces[0])
    for cut in pieces[1:]:
        gain = gain * one(*cut)
    return gain


def centred(stream_key, dims, width, bound, shards=(), held_as=jnp.bfloat16):
    entries = jax.random.normal(stream_key, dims, jnp.float32) * width
    if len(shards) > 0:
        entries = block_levels(stream_key, dims, shards, -0.22, 0.18) * entries
    return jnp.clip(entries, min=-bound, max=bound).astype(held_as)


def setup_inputs(seed: int = 0) -> dict:
    seeds = jax.random.split(jax.random.key(seed), 4)
    inverse = draw_inverse(jax.random.fold_in(seeds[3], 71), 0)
    right_side = centred(seeds[1], (GROUPS, K, PATHS), 1.0, 6.0, ((0, 4), (1, 8)), jnp.float32)
    penalty = jnp.clip(jnp.exp(jax.random.uniform(seeds[2], (PATHS,), jnp.float32, math.log(0.2), math.log(6.0))), 0.2, 6.0)
    return {"inverse": inverse, "right_side": right_side, "penalty": penalty}


def soft_shrink(values, limit):
    return jnp.sign(values) * jnp.maximum(jnp.abs(values) - limit, 0.0)


def group_product(pair):
    return jnp.dot(pair[0], pair[1], preferred_element_type=jnp.float32)


def reference(inverse, right_side, penalty):
    consensus = jnp.zeros((K, PATHS), jnp.float32)
    duals = jnp.zeros((GROUPS, K, PATHS), jnp.float32)
    limit = penalty / GROUPS
    for step in range(ITERS):
        shifted = (right_side + consensus[None] - duals).astype(jnp.bfloat16)
        primal = lax.map(group_product, (inverse, shifted))
        blended = jnp.sum(primal + duals, axis=0) / GROUPS
        consensus = soft_shrink(blended, limit[None, :])
        duals = duals + primal - consensus[None]
    return consensus, duals
```

```python
import functools

import jax
import jax.numpy as jnp
from jax import lax
from jax.experimental import pallas as pl
from jax.experimental.pallas import tpu as pltpu
from jax.sharding import PartitionSpec as P

ITERS = 3
FULL_SUMS = 1
LANES = 128
ROUTES = 2
MESH = pl.DeviceIdType.MESH


def gather_plan(bits):
    orders, events = [], []
    for route in range(ROUTES):
        network = list(range(1, bits))
        order = (network if route == 0 else network[::-1]) + [0]
        orders.append(order)
        for place in range(1 << bits):
            mask = sum(1 << order[j] for j in range(bits) if place >> j & 1)
            crossed = place & ((1 << (bits - 1)) - 1)
            other_core = place >> (bits - 1)
            key = 2 * crossed + (3 if crossed else 1) * other_core
            events.append((key, route, mask, place.bit_length()))
    events.sort()
    return orders, [event[1:] for event in events]


def kernel(
    cols, groups, inverse, right_side, penalty, consensus_out, duals_out,
    held, pieces, acc, total_in, duals, right, limit,
    from_low, from_high, to_high, to_low,
    low_rest, high_rest, up_rest, down_rest,
    load_sem, send_sem, recv_sem, up_send, up_recv, down_send, down_recv,
    up_rest_send, up_rest_recv, down_rest_send, down_rest_recv,
):
    rows = right_side.shape[0]
    halves = right_side.shape[1] // LANES
    phases = halves * ITERS
    coarse = phases - low_rest.shape[0]
    width = rows // ROUTES
    chunks, chunk = total_in.shape[1], total_in.shape[3]
    bits = cols.bit_length() - 1
    orders, events = gather_plan(bits)
    last_network = max(i for i, (_, mask, _) in enumerate(events) if not mask & 1)
    me = lax.axis_index("col")
    grp = lax.axis_index("grp")

    def load(source):
        return pltpu.make_async_copy(
            inverse.at[pl.ds(pl.multiple_of(source * rows, rows), rows), :],
            held.at[source],
            load_sem.at[source],
        )

    seen = []
    for _, mask, _ in events:
        if mask not in seen:
            seen.append(mask)
    for mask in seen:
        load(me ^ mask).start()

    barrier = pltpu.get_barrier_semaphore()
    for bit in range(bits):
        pl.semaphore_signal(barrier, inc=1, device_id={"col": me ^ (1 << bit)}, device_id_type=MESH)

    @pl.when(grp > 0)
    def _():
        pl.semaphore_signal(barrier, inc=1, device_id={"grp": grp - 1}, device_id_type=MESH)

    @pl.when(grp < groups - 1)
    def _():
        pl.semaphore_signal(barrier, inc=1, device_id={"grp": grp + 1}, device_id_type=MESH)

    for half in range(halves):
        for j in range(rows // LANES):
            right[half, :, j * LANES:(j + 1) * LANES] = (
                right_side[j * LANES:(j + 1) * LANES, half * LANES:(half + 1) * LANES].T
            )
        limit[half] = jnp.broadcast_to(
            penalty[0:1, half * LANES:(half + 1) * LANES], (LANES, LANES)
        ).T * (1.0 / groups)
        duals[half] = jnp.zeros((LANES, rows), jnp.float32)
        for route in range(ROUTES):
            pieces[half, me, route] = right[half, :, route * width:(route + 1) * width].astype(jnp.bfloat16)

    @pl.when(grp == 0)
    def _():
        from_low[...] = jnp.zeros_like(from_low)
        low_rest[...] = jnp.zeros_like(low_rest)

    @pl.when(grp == groups - 1)
    def _():
        from_high[...] = jnp.zeros_like(from_high)
        high_rest[...] = jnp.zeros_like(high_rest)

    below = jnp.minimum(grp, 1)
    above = jnp.minimum(groups - 1 - grp, 1)
    pl.semaphore_wait(barrier, bits + below + above)

    def hop(t, route, mask, bit):
        block = pieces.at[t, me ^ mask, route]
        return pltpu.make_async_remote_copy(
            src_ref=block,
            dst_ref=block,
            send_sem=send_sem.at[t, route, mask ^ (1 << bit)],
            recv_sem=recv_sem.at[t, route, mask ^ (1 << bit)],
            device_id={"col": me ^ (1 << bit)},
            device_id_type=MESH,
        )

    def arrival(t, route, mask):
        block = pieces.at[t, me ^ mask, route]
        return pltpu.make_async_remote_copy(
            src_ref=block,
            dst_ref=block,
            send_sem=send_sem.at[t, route, mask],
            recv_sem=recv_sem.at[t, route, mask],
            device_id={"col": me ^ 1},
            device_id_type=MESH,
        )

    def start_gather(t):
        stages = list(range(bits))
        for stage in [0] + stages[-1:] + stages[1:-1]:
            for route in range(ROUTES):
                hop(t, route, 0, orders[route][stage]).start()

    def up(t, c):
        return pltpu.make_async_remote_copy(
            src_ref=to_high.at[t, c], dst_ref=from_low.at[t, c],
            send_sem=up_send.at[t, c], recv_sem=up_recv.at[t, c],
            device_id={"grp": lax.rem(grp + 1, groups)}, device_id_type=MESH,
        )

    def down(t, c):
        return pltpu.make_async_remote_copy(
            src_ref=to_low.at[t, c], dst_ref=from_high.at[t, c],
            send_sem=down_send.at[t, c], recv_sem=down_recv.at[t, c],
            device_id={"grp": lax.rem(grp + groups - 1, groups)}, device_id_type=MESH,
        )

    def up_more(t, c):
        return pltpu.make_async_remote_copy(
            src_ref=up_rest.at[t - coarse, c], dst_ref=low_rest.at[t - coarse, c],
            send_sem=up_rest_send.at[t - coarse, c], recv_sem=up_rest_recv.at[t - coarse, c],
            device_id={"grp": lax.rem(grp + 1, groups)}, device_id_type=MESH,
        )

    def down_more(t, c):
        return pltpu.make_async_remote_copy(
            src_ref=down_rest.at[t - coarse, c], dst_ref=high_rest.at[t - coarse, c],
            send_sem=down_rest_send.at[t - coarse, c], recv_sem=down_rest_recv.at[t - coarse, c],
            device_id={"grp": lax.rem(grp + groups - 1, groups)}, device_id_type=MESH,
        )

    going_up = (up, up_more, from_low, low_rest, to_high, up_rest)
    going_down = (down, down_more, from_high, high_rest, to_low, down_rest)

    def send_sum(t, c, value, way):
        head_copy, rest_copy, _, _, head_out, rest_out = way
        head = value.astype(jnp.bfloat16)
        head_out[t, c] = head
        head_copy(t, c).start()

        @pl.when(t >= coarse)
        def _():
            rest_out[t - coarse, c] = (value - head.astype(jnp.float32)).astype(jnp.bfloat16)
            rest_copy(t, c).start()

    def forward_sum(t, c, half, way):
        head_copy, rest_copy, head_in, rest_in, _, _ = way
        head_copy(t, c).wait_recv()

        @pl.when(t >= coarse)
        def _():
            rest_copy(t, c).wait_recv()
            send_sum(t, c, head_in[t, c].astype(jnp.float32) + rest_in[t - coarse, c].astype(jnp.float32) + total_in[half, c], way)

        @pl.when(t < coarse)
        def _():
            send_sum(t, c, head_in[t, c].astype(jnp.float32) + total_in[half, c], way)

    def end_sum(t, c, way):
        head_copy, rest_copy = way[:2]
        head_copy(t, c).wait_recv()

        @pl.when(t >= coarse)
        def _():
            rest_copy(t, c).wait_recv()

    def start_sum(t):
        half = lax.rem(t, halves)

        @pl.when(jnp.logical_and(grp == 0, grp < groups - 1))
        def _():
            for c in range(chunks):
                send_sum(t, c, total_in[half, c], going_up)

        @pl.when(jnp.logical_and(grp == groups - 1, grp > 0))
        def _():
            for c in range(chunks):
                send_sum(t, c, total_in[half, c], going_down)

    lag = min(3, chunks)
    slots = chunks + lag * (groups - 3) if groups > 2 else 0

    def pass_on(t, slot):
        half = lax.rem(t, halves)
        c_up = slot - lag * (grp - 1)
        c_down = slot - lag * (groups - 2 - grp)
        inner = jnp.logical_and(grp > 0, grp < groups - 1)

        @pl.when(jnp.logical_and(inner, jnp.logical_and(c_up >= 0, c_up < chunks)))
        def _():
            forward_sum(t, c_up, half, going_up)

        @pl.when(jnp.logical_and(inner, jnp.logical_and(c_down >= 0, c_down < chunks)))
        def _():
            forward_sum(t, c_down, half, going_down)

    def finish_sum(t):
        @pl.when(jnp.logical_and(grp == groups - 1, grp > 0))
        def _():
            for c in range(chunks):
                end_sum(t, c, going_up)

        @pl.when(jnp.logical_and(grp == 0, grp < groups - 1))
        def _():
            for c in range(chunks):
                end_sum(t, c, going_down)

    def update(t, half):
        @pl.when(t >= coarse)
        def _():
            update_with(t, half, True)

        @pl.when(t < coarse)
        def _():
            update_with(t, half, False)

    def update_with(t, half, with_rest):
        last = t >= phases - halves
        for c in range(chunks):
            for part in range(chunk // LANES):
                inside = slice(part * LANES, (part + 1) * LANES)
                at = c * chunk + part * LANES
                own = total_in[half, c, :, inside]
                summed = (
                    own
                    + from_low[t, c, :, inside].astype(jnp.float32)
                    + from_high[t, c, :, inside].astype(jnp.float32)
                )
                if with_rest:
                    summed = (
                        summed
                        + low_rest[t - coarse, c, :, inside].astype(jnp.float32)
                        + high_rest[t - coarse, c, :, inside].astype(jnp.float32)
                    )
                blended = summed * (1.0 / groups)
                bound = limit[half]
                consensus = blended - jnp.minimum(jnp.maximum(blended, -bound), bound)
                dual = own - consensus
                duals[half, :, at:at + LANES] = dual
                shifted = (right[half, :, at:at + LANES] + consensus - dual).astype(jnp.bfloat16)

                @pl.when(jnp.logical_not(last))
                def _():
                    pieces[t + halves, me, at // width, :, at % width:at % width + LANES] = shifted

                @pl.when(last)
                def _():
                    acc[:, at:at + LANES] = consensus

    def write_out(half):
        for j in range(rows // LANES):
            down_rows = slice(j * LANES, (j + 1) * LANES)
            paths = slice(half * LANES, (half + 1) * LANES)
            consensus_out[down_rows, paths] = acc[:, down_rows].T
            duals_out[down_rows, paths] = duals[half, :, down_rows].T

    start_gather(0)

    def phase(t, carry):
        half = lax.rem(t, halves)
        slot = 0
        for i, (route, mask, stage) in enumerate(events):
            if mask:
                arrival(t, route, mask).wait_recv()
                for later in range(stage, bits):
                    hop(t, route, mask, orders[route][later]).start()
            if i == last_network:
                @pl.when(t < halves - 1)
                def _():
                    start_gather(t + 1)
            if mask not in [event[1] for event in events[:i]]:
                @pl.when(t == 0)
                def _():
                    load(me ^ mask).wait()
            source = me ^ mask
            product = jnp.dot(
                pieces[t, source, route],
                held[source, route * width:(route + 1) * width, :],
                preferred_element_type=jnp.float32,
            )
            if i == 0:
                acc[...] = product
            else:
                acc[...] += product
            due = slots * (i + 1) // max(1, last_network)
            while slot < min(due, slots):
                @pl.when(t > 0)
                def _(slot=slot):
                    pass_on(t - 1, slot)
                slot += 1
        for c in range(chunks):
            at = slice(c * chunk, (c + 1) * chunk)
            total_in[half, c] = acc[:, at] + duals[half, :, at]
        start_sum(t)

        @pl.when(t > 0)
        def _():
            earlier = lax.rem(t - 1, halves)
            finish_sum(t - 1)
            update(t - 1, earlier)

        @pl.when(jnp.logical_and(t >= halves - 1, t < phases - 1))
        def _():
            start_gather(t + 1)

        @pl.when(t == phases - 1)
        def _():
            write_out(halves - 2)

        return carry

    lax.fori_loop(0, phases, phase, 0)
    for slot in range(slots):
        pass_on(phases - 1, slot)
    finish_sum(phases - 1)
    update(phases - 1, halves - 1)
    write_out(halves - 1)

    def drain(t, carry):
        for route in range(ROUTES):
            for mask in range(1, cols):
                arrival(t, route, mask).wait_send()
        for c in range(chunks):
            @pl.when(grp < groups - 1)
            def _():
                up(t, c).wait_send()

                @pl.when(t >= coarse)
                def _():
                    up_more(t, c).wait_send()

            @pl.when(grp > 0)
            def _():
                down(t, c).wait_send()

                @pl.when(t >= coarse)
                def _():
                    down_more(t, c).wait_send()
        return carry

    lax.fori_loop(0, phases, drain, 0)


def on_device(cols, groups, inverse, right_side, penalty):
    rows, paths = right_side.shape[1:]
    halves = paths // LANES
    phases = halves * ITERS
    chunks = rows // LANES if rows >= 4 * LANES else 1
    chunk = rows // chunks
    whole = pl.BlockSpec(memory_space=pltpu.VMEM)
    fine = halves * FULL_SUMS
    sums = pltpu.VMEM((phases, chunks, LANES, chunk), jnp.bfloat16)
    rests = pltpu.VMEM((fine, chunks, LANES, chunk), jnp.bfloat16)
    consensus, duals = pl.pallas_call(
        functools.partial(kernel, cols, groups),
        out_shape=(
            jax.ShapeDtypeStruct((rows, paths), jnp.float32),
            jax.ShapeDtypeStruct((rows, paths), jnp.float32),
        ),
        in_specs=[pl.BlockSpec(memory_space=pl.ANY), whole, whole],
        out_specs=(whole, whole),
        scratch_shapes=[
            pltpu.VMEM((cols, rows, rows), jnp.bfloat16),
            pltpu.VMEM((phases, cols, ROUTES, LANES, rows // ROUTES), jnp.bfloat16),
            pltpu.VMEM((LANES, rows), jnp.float32),
            pltpu.VMEM((halves, chunks, LANES, chunk), jnp.float32),
            pltpu.VMEM((halves, LANES, rows), jnp.float32),
            pltpu.VMEM((halves, LANES, rows), jnp.float32),
            pltpu.VMEM((halves, LANES, LANES), jnp.float32),
            sums, sums, sums, sums,
            rests, rests, rests, rests,
            pltpu.SemaphoreType.DMA((cols,)),
            pltpu.SemaphoreType.DMA((phases, ROUTES, cols)),
            pltpu.SemaphoreType.DMA((phases, ROUTES, cols)),
            pltpu.SemaphoreType.DMA((phases, chunks)),
            pltpu.SemaphoreType.DMA((phases, chunks)),
            pltpu.SemaphoreType.DMA((phases, chunks)),
            pltpu.SemaphoreType.DMA((phases, chunks)),
            pltpu.SemaphoreType.DMA((fine, chunks)),
            pltpu.SemaphoreType.DMA((fine, chunks)),
            pltpu.SemaphoreType.DMA((fine, chunks)),
            pltpu.SemaphoreType.DMA((fine, chunks)),
        ],
        compiler_params=pltpu.CompilerParams(
            collective_id=0, has_side_effects=True, vmem_limit_bytes=60 * 1024 * 1024
        ),
    )(inverse[0], right_side[0], penalty[None, :])
    return consensus, duals[None]


def solution(mesh):
    in_specs = (P("grp", None, "col"), P("grp", "col", None), P())
    out_specs = (P("col", None), P("grp", "col", None))
    return jax.shard_map(
        functools.partial(on_device, mesh.shape["col"], mesh.shape["grp"]),
        mesh=mesh, in_specs=in_specs, out_specs=out_specs, check_vma=False,
    )
```
